256 devices in a mesh: edp: 8 (over z_lo, x), ep: 32 (over y, z_hi, core).
Axes of the slice: x: 4, y: 4, z: 8 (z_hi: 4, z_lo: 2; z = z_hi * 2 + z_lo), core: 2. Of those that a mesh axis runs over, the one named last changes fastest.
Arguments:
- attn_input: bfloat16 [32768, 3584], P(('edp', 'ep')), may hold values from -24 to 24
- kv_gain: float32 [3584], replicated, may hold values from 0.25 to 1.75
- latent_cot: bfloat16 [32768, 512], P(('edp', 'ep')), may hold values from -0.03125 to 0.03125
- attn_resid: float32 [3584, 512], P(('edp', 'ep')), may hold values from -4 to 4
- moe_input: bfloat16 [32768, 3584], P(('edp', 'ep')), may hold values from -24 to 24
- moe_cot: bfloat16 [32768, 3584], P(('edp', 'ep')), may hold values from -0.0625 to 0.0625
- expert_ids: int32 [32768, 2], P(('edp', 'ep')), may hold values from 0 to 7, all different within a row; in each aligned block of 128 rows (0 to 127, 128 to 255, ...) at most 40 rows name the same one
- gate_probs: float32 [32768, 2], P(('edp', 'ep')), may hold values from 0.2 to 1
- w_gate: bfloat16 [3584, 8192], P(None, 'ep'), may hold values from -0.09375 to 0.09375
- w_up: bfloat16 [3584, 8192], P(None, 'ep'), may hold values from -0.09375 to 0.09375
- w_down: bfloat16 [8192, 3584], P('ep'), may hold values from -0.1875 to 0.1875
- gate_resid: float32 [3584, 8192], P('edp', 'ep'), may hold values from -4 to 4
- up_resid: float32 [3584, 8192], P('edp', 'ep'), may hold values from -4 to 4
- down_resid: float32 [8192, 3584], P('ep', 'edp'), may hold values from -4 to 4
Outputs:
- kv_grad: bfloat16 [3584, 512], P(('edp', 'ep'))
- gate_grad: bfloat16 [3584, 8192], P('edp', 'ep')
- up_grad: bfloat16 [3584, 8192], P('edp', 'ep')
- down_grad: bfloat16 [8192, 3584], P('ep', 'edp')
The draws below stay inside these ranges and needn't reach their ends.
Inputs may be any that keep to these rules, and one draw needn't show every extreme that they name: `expert_ids`: each row names 2 different experts. Among the rows of one device no expert is named more than 40 times, and in some devices' rows one is named exactly 40 times.
All inputs are finite; a program needn't handle non-finite values.
Results may differ from the reference program's by a relative error of at most 0.019.
Values may be sent and summed in bfloat16 or wider, within the bound.
A program may use at most 128 MiB of HBM per device.

```python
import math
import jax
import jax.numpy as jnp
import numpy as np
from jax import lax

D = 3584
FH = 1024
KVL = 512
TOP = 2
TOK_DEV = 128
EXPERTS = 8
CAP = 40
TOKENS = 32768
N_EDP = 8
N_EP = 32


def strengthened(array, stream_key, source, target, shards_of, factor):
    def block_of(dim):
        return (jnp.arange(array.shape[dim]) // (array.shape[dim] // shards_of)).reshape((-1,) + (1,) * (array.ndim - 1 - dim))

    one_side = jax.random.permutation(stream_key, shards_of)[block_of(target)]
    second = (block_of(target) + shards_of // 2) % shards_of
    return jnp.where((block_of(source) == one_side) | (block_of(source) == second), factor * array, array)


def shard_levels(stream_key, shape, pieces, low, high):
    gain, own = 1.0, jax.random.fold_in(stream_key, 6)
    for axis_at, blocks in pieces:
        steps = jnp.exp(jax.random.uniform(jax.random.fold_in(own, axis_at), (blocks,), jnp.float32, low / len(pieces), high / len(pieces)))
        gain = gain * jnp.repeat(steps, shape[axis_at] // blocks).reshape([-1 if axis == axis_at else 1 for axis in range(len(shape))])
    return gain


def routed_block(key, own, number, rows, number_of, top, limit, skew):
    sequence = jax.random.permutation(key, number_of)
    crowded, usual = load_shares(number_of, rows * top, limit, skew, True), load_shares(number_of, rows * top, limit, skew, False)
    places = jnp.arange(number_of)

    def named(lengths, offset_by):
        used = int((lengths > 0).sum())
        fixed = max(1, used // 4)
        shifted = fixed + (places - fixed + offset_by * (used - fixed)) % max(1, number_of - fixed)
        return jnp.zeros((number_of,), jnp.int32).at[sequence[jnp.where(places < fixed, places, shifted)]].set(jnp.asarray(lengths, jnp.int32))

    lengths = jnp.where(number % 4 == 0, named(crowded, number // 4), named(usual, number - number // 4 - 1))
    mixed = jax.random.permutation(jax.random.fold_in(own, 3), number_of)
    donor, receiver = mixed[0:number_of // 2 * 2:2], mixed[1:number_of // 2 * 2:2]
    margin = jnp.minimum(lengths[donor] - 1, limit - lengths[receiver]) // 2
    margin = jnp.where((donor == sequence[0]) | (receiver == sequence[0]) | (lengths[receiver] == 0), 0, jnp.maximum(margin, 0))
    shifted = jax.random.randint(jax.random.fold_in(own, 4), (number_of // 2,), 0, 1 << 20) % (margin + 1)
    lengths = lengths.at[donor].add(-shifted).at[receiver].add(shifted)
    items = jnp.searchsorted(jnp.cumsum(lengths), jnp.arange(rows * top), side="right").astype(jnp.int32)
    grid = items.reshape(top, rows).T
    grid = grid[jax.random.permutation(jax.random.fold_in(own, 1), rows)]
    offset_by = jax.random.randint(jax.random.fold_in(own, 2), (rows, 1), 0, top)
    return jnp.take_along_axis(grid, (jnp.arange(top)[None, :] + offset_by) % top, axis=1)


def load_shares(amount, total, reach, skew, full):
    weights = [(1 << 20) // math.isqrt(rank ** skew) + 1 for rank in range(1, amount + 1)]
    largest = reach if full else min(reach, max(-(-total // amount), total * weights[0] // sum(weights)))
    least = 1 if total - largest >= amount - 1 else 0
    counts, rest = [largest] + [least] * (amount - 1), total - largest - least * (amount - 1)
    while rest > 0:
        candidates = [i for i in range(1, amount) if counts[i] < largest] or [i for i in range(1, amount) if counts[i] < reach]
        pool, remaining = sum([weights[i] for i in candidates]), rest
        for i in candidates:
            extra = min(reach - counts[i], max(1, remaining * weights[i] // pool), rest)
            counts[i] = counts[i] + extra
            rest = rest - extra
    return np.array(counts)


def noise(stream_key, extent, scale, reach, shards=(), held_as=jnp.bfloat16):
    drawn = scale * jax.random.normal(stream_key, extent, jnp.float32)
    if shards:
        drawn = drawn * shard_levels(stream_key, extent, shards, -0.22, 0.18)
    return jnp.clip(drawn, -reach, reach).astype(held_as)


def heavy_noise(stream_key, dims, width, reach, pieces, heavy, held_as=jnp.bfloat16):
    entries = width * jax.random.normal(stream_key, dims, jnp.float32)
    if pieces:
        entries = entries * shard_levels(stream_key, dims, pieces, -0.22, 0.18)
    return jnp.clip(strengthened(entries, jax.random.fold_in(stream_key, 3), *heavy), -reach, reach).astype(held_as)


def setup_inputs(seed: int = 0) -> dict:
    seeds = jax.random.split(jax.random.key(seed), 15)
    attn_input = heavy_noise(seeds[0], (TOKENS, D), 1.0, 24.0, ((0, 256),), (0, 1, 256, 6.0))
    kv_gain = jnp.clip(1.0 + 0.15 * jax.random.normal(seeds[1], (D,), jnp.float32), 0.25, 1.75)
    latent_cot = noise(seeds[2], (TOKENS, KVL), TOKENS ** -0.5, 0.03125, ((0, 256),))
    attn_resid = noise(seeds[3], (D, KVL), 0.25, 4.0, ((0, 256),), jnp.float32)
    moe_input = heavy_noise(seeds[4], (TOKENS, D), 1.0, 24.0, ((0, 256),), (0, 1, 256, 6.0))
    moe_cot = noise(seeds[5], (TOKENS, D), (TOKENS * TOP // EXPERTS) ** -0.5, 0.0625, ((0, 256),))
    expert_ids_keys = jax.random.split(jax.random.fold_in(seeds[6], 1), TOKENS // TOK_DEV)
    expert_ids_turns = jax.random.permutation(jax.random.fold_in(seeds[6], 3), TOKENS // TOK_DEV)
    expert_ids = jax.vmap(lambda own, number: routed_block(jax.random.fold_in(seeds[6], 2), own, number, TOK_DEV, EXPERTS, TOP, CAP, 1))(expert_ids_keys, expert_ids_turns).reshape((TOKENS, TOP))
    gate_probs = jnp.clip(0.2 + 0.8 * jax.random.uniform(seeds[7], (TOKENS, TOP), jnp.float32) ** shard_levels(seeds[7], (TOKENS, TOP), ((0, 256),), -0.2, 0.2), 0.2, 1.0)
    w_gate = noise(seeds[8], (D, EXPERTS * FH), D ** -0.5, 0.09375, ((1, 32),))
    w_up = noise(seeds[9], (D, EXPERTS * FH), D ** -0.5, 0.09375, ((1, 32),))
    w_down = noise(seeds[10], (EXPERTS * FH, D), FH ** -0.5, 0.1875, ((0, 32),))
    gate_resid = noise(seeds[11], (D, EXPERTS * FH), 0.25, 4.0, ((0, 8), (1, 32)), jnp.float32)
    up_resid = noise(seeds[12], (D, EXPERTS * FH), 0.25, 4.0, ((0, 8), (1, 32)), jnp.float32)
    down_resid = noise(seeds[13], (EXPERTS * FH, D), 0.25, 4.0, ((0, 32), (1, 8)), jnp.float32)
    return dict(attn_input=attn_input, kv_gain=kv_gain, latent_cot=latent_cot, attn_resid=attn_resid, moe_input=moe_input, moe_cot=moe_cot, expert_ids=expert_ids, gate_probs=gate_probs, w_gate=w_gate, w_up=w_up, w_down=w_down, gate_resid=gate_resid, up_resid=up_resid, down_resid=down_resid)


epsilon = 1e-06

def contract_rows(left, right):
    return lax.dot_general(left, right, (((0,), (0,)), ((), ())), preferred_element_type=jnp.float32)

def slot_tables(expert_ids, gate_probs):
    labels = jnp.arange(EXPERTS, dtype=jnp.int32)
    one_hot = (expert_ids[:, :, None] == labels[None, None, :]).astype(jnp.int32)
    chosen = lax.optimization_barrier(jnp.sum(one_hot, axis=1))
    weight = lax.optimization_barrier(jnp.sum(one_hot.astype(jnp.float32) * gate_probs[:, :, None], axis=1))
    position = jnp.cumsum(chosen, axis=0) - chosen
    slot_ids = jnp.arange(CAP, dtype=jnp.int32)
    dispatch = (chosen[None, :, :] > 0) & (position[None, :, :] == slot_ids[:, None, None])
    return (jnp.transpose(dispatch, (2, 0, 1)).astype(jnp.float32), weight)

def device_slots(inputs, cots, expert_ids, gate_probs):
    dispatch, weight = slot_tables(expert_ids, gate_probs)
    sent_in = jnp.einsum('ect,td->ecd', dispatch, inputs.astype(jnp.float32)).astype(jnp.bfloat16)
    sent_cot = jnp.einsum('ect,td->ecd', dispatch, cots.astype(jnp.float32))
    slot_weight = jnp.einsum('ect,te->ec', dispatch, weight)
    return (sent_in, (sent_cot * slot_weight[:, :, None]).astype(jnp.bfloat16))

def group_terms(inputs, cots, expert_ids, gate_probs, w_gate, w_up, w_down):
    sent_in, sent_cot = jax.vmap(device_slots)(inputs, cots, expert_ids, gate_probs)

    def per_expert(index):
        rows_in = lax.dynamic_index_in_dim(sent_in, index, 1, keepdims=False).reshape(N_EP * CAP, D)
        rows_cot = lax.dynamic_index_in_dim(sent_cot, index, 1, keepdims=False).reshape(N_EP * CAP, D)
        gate_cols = lax.dynamic_slice_in_dim(w_gate, index * FH, FH, 1)
        up_cols = lax.dynamic_slice_in_dim(w_up, index * FH, FH, 1)
        down_rows = lax.dynamic_slice_in_dim(w_down, index * FH, FH, 0)
        gate_proj = jnp.dot(rows_in, gate_cols, preferred_element_type=jnp.float32)
        up_proj = jnp.dot(rows_in, up_cols, preferred_element_type=jnp.float32)
        sigmoid_gate = jax.nn.sigmoid(gate_proj)
        active = (gate_proj * sigmoid_gate * up_proj).astype(jnp.bfloat16)
        back_grad = lax.dot_general(rows_cot, down_rows, (((1,), (1,)), ((), ())), preferred_element_type=jnp.float32)
        up_rows = (back_grad * gate_proj * sigmoid_gate).astype(jnp.bfloat16)
        gate_rows = (back_grad * up_proj * sigmoid_gate * (1.0 + gate_proj * (1.0 - sigmoid_gate))).astype(jnp.bfloat16)
        return (contract_rows(rows_in, gate_rows).astype(jnp.bfloat16), contract_rows(rows_in, up_rows).astype(jnp.bfloat16), contract_rows(active, rows_cot).astype(jnp.bfloat16))
    return lax.map(per_expert, jnp.arange(EXPERTS, dtype=jnp.int32))

def reference(attn_input, kv_gain, latent_cot, attn_resid, moe_input, moe_cot, expert_ids, gate_probs, w_gate, w_up, w_down, gate_resid, up_resid, down_resid):
    values = attn_input.astype(jnp.float32)
    inv_rms = lax.rsqrt(lax.optimization_barrier(jnp.mean(values * values, axis=1, keepdims=True)) + epsilon)
    normed = (values * inv_rms * kv_gain[None, :]).astype(jnp.bfloat16)
    kv_grad = (contract_rows(normed, latent_cot) + attn_resid).astype(jnp.bfloat16)
    groups = (moe_input.reshape(N_EDP, N_EP, TOK_DEV, D), moe_cot.reshape(N_EDP, N_EP, TOK_DEV, D), expert_ids.reshape(N_EDP, N_EP, TOK_DEV, TOP), gate_probs.reshape(N_EDP, N_EP, TOK_DEV, TOP))

    def accumulate(carry, group):
        terms = group_terms(group[0], group[1], group[2], group[3], w_gate, w_up, w_down)
        return ((carry[0] + terms[0].astype(jnp.float32), carry[1] + terms[1].astype(jnp.float32), carry[2] + terms[2].astype(jnp.float32)), None)
    start = (jnp.zeros((EXPERTS, D, FH), jnp.float32), jnp.zeros((EXPERTS, D, FH), jnp.float32), jnp.zeros((EXPERTS, FH, D), jnp.float32))
    sums, _ = lax.scan(accumulate, start, groups)
    gate_sum = jnp.transpose(sums[0], (1, 0, 2)).reshape(D, EXPERTS * FH)
    up_sum = jnp.transpose(sums[1], (1, 0, 2)).reshape(D, EXPERTS * FH)
    down_sum = sums[2].reshape(EXPERTS * FH, D)
    gate_grad = (gate_sum + gate_resid).astype(jnp.bfloat16)
    up_grad = (up_sum + up_resid).astype(jnp.bfloat16)
    down_grad = (down_sum + down_resid).astype(jnp.bfloat16)
    return (kv_grad, gate_grad, up_grad, down_grad)
```

```python
import jax
import jax.numpy as jnp
from jax import lax
from jax.experimental import pallas as pl
from jax.experimental.pallas import tpu as pltpu
from jax.sharding import Mesh
from jax.sharding import PartitionSpec as P

MESH = pl.DeviceIdType.MESH
EDP_EP = ("edp_0", "edp_1", "ep_0", "ep_1", "ep_2")
EP = ("ep_0", "ep_1", "ep_2")
EDP = ("edp_0", "edp_1")
F32, BF16 = jnp.float32, jnp.bfloat16

epsilon = 1e-06

D, TOK, FQ, CAP, KVL = 3584, 128, 256, 40, 512
EXPERTS = 8
BLOCK = 2 * CAP
CHUNK = 4 * BLOCK
ROWS = 4 * CHUNK
PIECES = 2
WIDE = D // PIECES
PAIR = 896
SLICE = 2688
COPIES = 96


def kernel(
    ids_ref,
    probs_ref,
    gain_ref,
    input_hbm,
    cot_hbm,
    attn_hbm,
    latent_hbm,
    w_gate_hbm,
    w_up_hbm,
    w_down_hbm,
    kv_out,
    terms_out,
    own,
    tokens,
    meta,
    ready,
    passing,
    rows,
    w_gate_up,
    w_down,
    latent,
    hidden_t,
    work,
    parts,
    first_sums,
    second_sums,
    last_sum,
    kv_core,
    kv_x,
    kv_x_sum,
    kv_y,
    kv_y_sum,
    kv_z,
    send_sems,
    recv_sems,
    load_sems,
):
    zl, x, y = lax.axis_index("edp_0"), lax.axis_index("edp_1"), lax.axis_index("ep_0")
    zh, c = lax.axis_index("ep_1"), lax.axis_index("ep_2")
    z = zh * 2 + zl
    other = 1 - c

    def at_z(target):
        return (lax.rem(target, 2), x, y, target // 2, c)

    def at_y(target):
        return (zl, x, target, zh, c)

    def at_x(target):
        return (zl, target, y, zh, c)

    other_core = (zl, x, y, zh, other)
    other_zl = (1 - zl, x, y, zh, c)

    used = [0]

    def remote(src, dst, device, index=None):
        if index is None:
            index = used[0]
            used[0] += 1
        return pltpu.make_async_remote_copy(
            src_ref=src,
            dst_ref=dst,
            send_sem=send_sems.at[index],
            recv_sem=recv_sems.at[index],
            device_id=device,
            device_id_type=MESH,
        )

    loads = [0]

    def local(src, dst):
        copy = pltpu.make_async_copy(src, dst, load_sems.at[loads[0]])
        loads[0] += 1
        return copy

    load_own = [local(input_hbm, own.at[0]), local(cot_hbm, own.at[1])]
    load_later = [
        local(w_gate_hbm, w_gate_up.at[:, pl.ds(0, FQ)]),
        local(w_up_hbm, w_gate_up.at[:, pl.ds(FQ, FQ)]),
        local(w_down_hbm, w_down),
    ]
    load_latent = local(latent_hbm, latent)
    for copy in load_own + load_later + [load_latent]:
        copy.start()

    barrier = pltpu.get_barrier_semaphore()
    partners = [other_core]
    partners += [at_z(lax.rem(z + step, 8)) for step in range(1, 8)]
    partners += [at_y(lax.rem(y + step, 4)) for step in range(1, 4)]
    partners += [at_x(lax.rem(x + step, 4)) for step in range(1, 4)]
    for partner in partners:
        pl.semaphore_signal(barrier, inc=1, device_id=partner, device_id_type=MESH)

    expert = lax.broadcasted_iota(jnp.int32, (EXPERTS, TOK), 0)
    first, second = ids_ref[0:1, :] == expert, ids_ref[1:2, :] == expert
    chosen = jnp.where(first | second, 1.0, 0.0)
    earlier = lax.broadcasted_iota(jnp.int32, (TOK, TOK), 0) < lax.broadcasted_iota(
        jnp.int32, (TOK, TOK), 1
    )
    position = jnp.dot(
        chosen.astype(BF16),
        jnp.where(earlier, 1.0, 0.0).astype(BF16),
        preferred_element_type=F32,
    )
    shift = (c * CAP).astype(F32)
    meta[0, c, 0:8, :] = jnp.where(first | second, position + shift, -1.0)
    meta[0, c, 8:16, :] = jnp.where(first, probs_ref[0:1, :], 0.0) + jnp.where(
        second, probs_ref[1:2, :], 0.0
    )

    pl.semaphore_wait(barrier, len(partners))

    mine = pl.ds(pl.multiple_of(c * TOK, TOK), TOK)
    theirs = pl.ds(pl.multiple_of(other * TOK, TOK), TOK)
    for copy in load_own:
        copy.wait()
    swap = remote(own.at[other], tokens.at[0, mine], other_core)
    swap.start()
    swap_in = remote(own.at[other], tokens.at[0, theirs], other_core, used[0] - 1)
    swap_meta = remote(meta.at[0, c], meta.at[0, c], other_core)
    swap_meta.start()
    swap_meta_in = remote(meta.at[0, other], meta.at[0, other], other_core, used[0] - 1)
    keep = local(own.at[c], tokens.at[0, mine])
    keep.start()
    swap_meta_in.wait_recv()
    swap_in.wait_recv()
    keep.wait()

    even = 1 - lax.rem(z, 2)
    near = lax.rem(z + 9 - 2 * even, 8)
    far = lax.rem(z + 4 * even + 6, 8)
    columns = [pl.ds(piece * WIDE, WIDE) for piece in range(PIECES)]

    def along_z(source, slot, target):
        return [remote(meta.at[source], meta.at[slot], at_z(target))] + [
            remote(tokens.at[source, :, part], tokens.at[slot, :, part], at_z(target))
            for part in columns
        ]

    z_near, z_far = along_z(0, 1, near), along_z(0, 2, far)
    z_next = along_z(1, 3, far)
    arrival = [None, z_near, z_far, z_next]
    for one, two in zip(z_near, z_far):
        one.start()
        two.start()

    half = zh // 2
    up, down = lax.rem(y + 1, 4), lax.rem(y + 3, 4)
    onward = lax.rem(y + 1 + 2 * c, 4)
    slot_of = lax.broadcasted_iota(jnp.int32, (BLOCK, TOK), 0).astype(F32)
    core_weight = c.astype(F32)

    def block_rows(chunk, step):
        return pl.ds(chunk * CHUNK + step * BLOCK, BLOCK)

    y_sent, y_passed, core_sent, core_got = {}, {}, {}, {}
    for chunk in range(4):
        for piece in range(PIECES):
            part, slot = columns[piece], chunk % 2
            y_sent[chunk, piece] = [
                remote(
                    ready.at[slot, 0, :, part],
                    rows.at[c, block_rows(chunk, 1), part],
                    at_y(up),
                ),
                remote(ready.at[slot, 1, :, part], passing.at[chunk, :, part], at_y(onward)),
                remote(
                    ready.at[slot, 2, :, part],
                    rows.at[c, block_rows(chunk, 3), part],
                    at_y(down),
                ),
            ]
            y_passed[chunk, piece] = remote(
                passing.at[chunk, :, part],
                rows.at[c, block_rows(chunk, 2), part],
                at_y(onward),
            )
            whole = pl.ds(chunk * CHUNK, CHUNK)
            core_sent[chunk, piece] = remote(
                rows.at[c, whole, part], rows.at[c, whole, part], other_core
            )
            core_got[chunk, piece] = remote(
                rows.at[other, whole, part], rows.at[other, whole, part], other_core, used[0] - 1
            )

    def send_rows(chunk, piece):
        part = columns[piece]
        for step in (2, 1, 3, 0):
            name = lax.rem(y + step, 4) * 2 + half
            hot = [
                meta[chunk, core, pl.ds(name, 1), :] == slot_of for core in range(2)
            ]
            hot = [jnp.where(one, 1.0, 0.0) for one in hot]
            weight = sum(
                jnp.sum(one * meta[chunk, core, pl.ds(name + 8, 1), :], axis=1, keepdims=True)
                for core, one in enumerate(hot)
            )
            scale = weight * core_weight + (1.0 - core_weight)
            picked = jnp.dot(
                jnp.concatenate(hot, axis=1).astype(BF16),
                tokens[chunk, :, part],
                preferred_element_type=F32,
            )
            picked = (picked * scale).astype(BF16)
            if step == 0:
                rows[c, block_rows(chunk, 0), part] = picked
            else:
                if chunk >= 2:
                    y_sent[chunk - 2, piece][step - 1].wait_send()
                ready[chunk % 2, step - 1, :, part] = picked
                y_sent[chunk, piece][step - 1].start()

    def pass_rows(chunk, piece):
        y_sent[chunk, piece][1].wait_recv()
        y_passed[chunk, piece].start()

    def share_rows(chunk, piece):
        y_sent[chunk, piece][0].wait_recv()
        y_sent[chunk, piece][2].wait_recv()
        y_passed[chunk, piece].wait_recv()
        core_sent[chunk, piece].start()

    for piece in range(PIECES):
        send_rows(0, piece)

    swap.wait_send()
    load_attn = local(attn_hbm, own.at[0])
    load_attn.start()
    load_latent.wait()
    load_attn.wait()

    @pl.loop(0, TOK // 16)
    def _(tile):
        part = pl.ds(pl.multiple_of(tile * 16, 16), 16)
        values = own[0, part, :].astype(F32)
        inv_rms = lax.rsqrt(jnp.mean(values * values, axis=1, keepdims=True) + epsilon)
        own[1, part, :] = (values * inv_rms * gain_ref[...]).astype(BF16)

    work[896:904, 0:KVL] = jnp.zeros((8, KVL), F32)

    @pl.loop(0, 4)
    def _(tile):
        normed = own[1, :, pl.ds(pl.multiple_of(tile * PAIR, 128), PAIR)]
        work[0:896, 0:KVL] = lax.dot_general(
            normed, latent[...], (((0,), (0,)), ((), ())), preferred_element_type=F32
        )
        start = lax.rem(tile, 2) * 4096 + (tile // 2) * 64
        for place in range(64):
            fixed = (place % 2) * 8192 + (place // 8) * 512 + (place % 8 // 2) * 128
            share = work[14 * place : 14 * place + 16, 0:KVL].astype(BF16)
            for lane in range(4):
                to = pl.multiple_of(start + fixed + lane * 16, 16)
                parts[pl.ds(to, 16), :] = share[:, lane * 128 : lane * 128 + 128]

    def half_of(core):
        return pl.multiple_of(core * 8192, 8192)

    kv_to_core = remote(parts.at[pl.ds(half_of(other), 8192)], kv_core, other_core)
    kv_to_core.start()

    for piece in range(PIECES):
        pass_rows(0, piece)

    kv_to_core.wait_recv()

    @pl.loop(0, 16)
    def _(tile):
        at = pl.multiple_of(tile * 512, 512)
        here = pl.ds(half_of(c) + at, 512)
        parts[here, :] = (
            parts[here, :].astype(F32) + kv_core[pl.ds(at, 512), :].astype(F32)
        ).astype(BF16)

    kv_to_x = []
    for step in range(1, 4):
        target = lax.rem(x + step, 4)
        at = pl.ds(half_of(c) + pl.multiple_of(target * 2048, 2048), 2048)
        kv_to_x.append(remote(parts.at[at], kv_x.at[step - 1], at_x(target)))
        kv_to_x[-1].start()

    for piece in range(PIECES):
        share_rows(0, piece)

    z_near[0].wait_recv()
    z_next[0].start()
    for piece in range(PIECES):
        z_near[1 + piece].wait_recv()
        z_next[1 + piece].start()
        send_rows(1, piece)

    for copy in kv_to_x:
        copy.wait()

    @pl.loop(0, 4)
    def _(tile):
        at = pl.multiple_of(tile * 512, 512)
        total = parts[pl.ds(half_of(c) + pl.multiple_of(x * 2048, 2048) + at, 512), :].astype(F32)
        for step in range(3):
            total = total + kv_x[step, pl.ds(at, 512), :].astype(F32)
        kv_x_sum[pl.ds(at, 512), :] = total.astype(BF16)

    kv_to_y = []
    for step in range(1, 4):
        target = lax.rem(y + step, 4)
        at = pl.ds(pl.multiple_of(target * 512, 512), 512)
        kv_to_y.append(remote(kv_x_sum.at[at], kv_y.at[step - 1], at_y(target)))
        kv_to_y[-1].start()

    for piece in range(PIECES):
        pass_rows(1, piece)
    for piece in range(PIECES):
        share_rows(1, piece)

    for copy in kv_to_y:
        copy.wait()
    total = kv_x_sum[pl.ds(pl.multiple_of(y * 512, 512), 512), :].astype(F32)
    for step in range(3):
        total = total + kv_y[step].astype(F32)
    kv_y_sum[...] = total.astype(BF16)
    kv_to_z = []
    for step in range(1, 8):
        target = lax.rem(z + step, 8)
        at = pl.ds(pl.multiple_of(target * 64, 64), 64)
        kv_to_z.append(remote(kv_y_sum.at[at], kv_z.at[step - 1], at_z(target)))
        kv_to_z[-1].start()

    z_far[0].wait_recv()
    for piece in range(PIECES):
        z_far[1 + piece].wait_recv()
        send_rows(2, piece)

    def hidden_units(part):
        for chunk in (2 * part, 2 * part + 1):
            for piece in range(PIECES):
                core_got[chunk, piece].wait_recv()
        group = pl.ds(part * 2 * CHUNK, 2 * CHUNK)
        tall = 2 * CHUNK
        work[0:tall, 0 : 3 * FQ] = jnp.zeros((tall, 3 * FQ), F32)

        @pl.loop(0, 7)
        def _(tile):
            at = pl.ds(pl.multiple_of(tile * 512, 512), 512)
            work[0:tall, 0 : 2 * FQ] += jnp.dot(
                rows[0, group, at], w_gate_up[at, :], preferred_element_type=F32
            )
            work[0:tall, 2 * FQ : 3 * FQ] += lax.dot_general(
                rows[1, group, at],
                w_down[:, at],
                (((1,), (1,)), ((), ())),
                preferred_element_type=F32,
            )

        @pl.loop(0, tall // 128)
        def _(tile):
            at = pl.ds(pl.multiple_of(tile * 128, 128), 128)
            to = pl.ds(pl.multiple_of(part * tall + tile * 128, 128), 128)
            gate, up_proj = work[at, 0:FQ], work[at, FQ : 2 * FQ]
            back = work[at, 2 * FQ : 3 * FQ]
            sigmoid = jax.nn.sigmoid(gate)
            active = gate * sigmoid * up_proj
            up_rows = back * gate * sigmoid
            gate_rows = back * up_proj * sigmoid * (1.0 + gate * (1.0 - sigmoid))
            hidden_t[0:FQ, to] = gate_rows.T.astype(BF16)
            hidden_t[FQ : 2 * FQ, to] = up_rows.T.astype(BF16)
            hidden_t[2 * FQ : 3 * FQ, to] = active.T.astype(BF16)

    for copy in load_later:
        copy.wait()
    hidden_units(0)

    for piece in range(PIECES):
        pass_rows(2, piece)
    for piece in range(PIECES):
        share_rows(2, piece)

    z_next[0].wait_recv()
    for piece in range(PIECES):
        z_next[1 + piece].wait_recv()
        send_rows(3, piece)

    for copy in kv_to_z:
        copy.wait()
    total = kv_y_sum[pl.ds(pl.multiple_of(z * 64, 64), 64), :].astype(F32)
    for step in range(7):
        total = total + kv_z[step].astype(F32)
    for lane in range(4):
        kv_out[:, lane * 128 : lane * 128 + 128] = total[lane * 16 : lane * 16 + 16, :]
    kv_to_core.wait_send()

    for piece in range(PIECES):
        pass_rows(3, piece)
    for piece in range(PIECES):
        share_rows(3, piece)
    hidden_units(1)

    right, left, across = lax.rem(x + 1, 4), lax.rem(x + 3, 4), lax.rem(x + 2, 4)

    def slice_at(which):
        return pl.ds(pl.multiple_of(which * SLICE, SLICE), SLICE)

    low = lax.broadcasted_iota(jnp.int32, (384, 128), 1) < 64

    def gradients(pair):
        at = pl.ds(pl.multiple_of(pair * PAIR, 128), PAIR)
        work[0 : 2 * FQ, :] = jnp.dot(
            hidden_t[0 : 2 * FQ, :], rows[0, :, at], preferred_element_type=F32
        )
        work[2 * FQ : 3 * FQ, :] = jnp.dot(
            hidden_t[2 * FQ : 3 * FQ, :], rows[1, :, at], preferred_element_type=F32
        )
        start = pair * 2 * SLICE

        def put(which, block, value):
            to = pl.multiple_of(start + which * SLICE + block * 384, 128)
            parts[pl.ds(to, 384), :] = value.astype(BF16)

        for lane in range(3):
            for tall in range(2):
                high = slice(tall * 384, tall * 384 + 384)
                put(0, tall * 3 + lane, work[high, lane * 128 : lane * 128 + 128])
                put(1, tall * 3 + lane, work[high, 512 + lane * 128 : 640 + lane * 128])
        top, bottom = work[0:384, 384:512], pltpu.roll(work[384:768, 384:512], 64, 1)
        put(0, 6, jnp.where(low, top, bottom))
        put(1, 6, jnp.where(low, bottom, top))

    side = x // 2
    gradients(1 - side)
    to_right = remote(parts.at[slice_at(across)], first_sums.at[0], at_x(right))
    to_right.start()
    gradients(3 - side)
    to_left = remote(parts.at[slice_at(4 + across)], first_sums.at[1], at_x(left))
    to_left.start()
    gradients(side)
    gradients(2 + side)
    plain_right = remote(parts.at[slice_at(4 + right)], second_sums.at[2], at_x(right))
    plain_left = remote(parts.at[slice_at(left)], second_sums.at[1], at_x(left))
    plain_right.start()
    plain_left.start()

    def add_into(which, *added):
        @pl.loop(0, 7)
        def _(tile):
            at = pl.multiple_of(tile * 384, 128)
            here = pl.ds(pl.multiple_of(which * SLICE, 128) + at, 384)
            total = parts[here, :].astype(F32)
            for one in added:
                total = total + one[pl.ds(at, 384), :].astype(F32)
            parts[here, :] = total.astype(BF16)

    to_right.wait_recv()
    add_into(right, first_sums.at[0])
    sum_right = remote(parts.at[slice_at(right)], second_sums.at[0], at_x(right))
    sum_right.start()
    to_left.wait_recv()
    add_into(4 + left, first_sums.at[1])
    sum_left = remote(parts.at[slice_at(4 + left)], second_sums.at[3], at_x(left))
    sum_left.start()

    for copy in (plain_right, plain_left, sum_right, sum_left):
        copy.wait_recv()
    far_half = 1 - zl
    add_into(far_half * 4 + x, second_sums.at[far_half * 2], second_sums.at[far_half * 2 + 1])
    to_zl = remote(parts.at[slice_at(far_half * 4 + x)], last_sum, other_zl)
    to_zl.start()
    to_zl.wait_recv()
    mine_at = pl.multiple_of((zl * 4 + x) * SLICE, 128)
    for block in range(7):
        at = pl.ds(block * 384, 384)
        total = parts[pl.ds(mine_at + block * 384, 384), :].astype(F32)
        total = total + second_sums[zl * 2, at, :].astype(F32)
        total = total + second_sums[zl * 2 + 1, at, :].astype(F32)
        work[0:384, block * 128 : block * 128 + 128] = total + last_sum[at, :].astype(F32)
    store = local(work.at[pl.ds(0, 384)], terms_out)
    store.start()

    for copy in (swap_meta, to_right, to_left, plain_right, plain_left, sum_right, sum_left, to_zl):
        copy.wait_send()
    for group in (z_near, z_far, z_next):
        for copy in group:
            copy.wait_send()
    for chunk in range(4):
        for piece in range(PIECES):
            if chunk >= 2:
                for copy in y_sent[chunk, piece]:
                    copy.wait_send()
            y_passed[chunk, piece].wait_send()
            core_sent[chunk, piece].wait_send()
    store.wait()


def run_kernel(ids, probs, gain, *arrays):
    vmem, any_space = pl.BlockSpec(memory_space=pltpu.VMEM), pl.BlockSpec(memory_space=pl.ANY)
    return pl.pallas_call(
        kernel,
        out_shape=(
            jax.ShapeDtypeStruct((16, KVL), F32),
            jax.ShapeDtypeStruct((384, PAIR), F32),
        ),
        in_specs=[vmem] * 3 + [any_space] * len(arrays),
        out_specs=(vmem, any_space),
        scratch_shapes=[
            pltpu.VMEM((2, TOK, D), BF16),
            pltpu.VMEM((4, 2 * TOK, D), BF16),
            pltpu.VMEM((4, 2, 16, TOK), F32),
            pltpu.VMEM((2, 3, BLOCK, D), BF16),
            pltpu.VMEM((4, BLOCK, D), BF16),
            pltpu.VMEM((2, ROWS, D), BF16),
            pltpu.VMEM((D, 2 * FQ), BF16),
            pltpu.VMEM((FQ, D), BF16),
            pltpu.VMEM((TOK, KVL), BF16),
            pltpu.VMEM((3 * FQ, ROWS), BF16),
            pltpu.VMEM((904, PAIR), F32),
            pltpu.VMEM((8 * SLICE, 128), BF16),
            pltpu.VMEM((2, SLICE, 128), BF16),
            pltpu.VMEM((4, SLICE, 128), BF16),
            pltpu.VMEM((SLICE, 128), BF16),
            pltpu.VMEM((8192, 128), BF16),
            pltpu.VMEM((3, 2048, 128), BF16),
            pltpu.VMEM((2048, 128), BF16),
            pltpu.VMEM((3, 512, 128), BF16),
            pltpu.VMEM((512, 128), BF16),
            pltpu.VMEM((7, 64, 128), BF16),
            pltpu.SemaphoreType.DMA((COPIES,)),
            pltpu.SemaphoreType.DMA((COPIES,)),
            pltpu.SemaphoreType.DMA((10,)),
        ],
        compiler_params=pltpu.CompilerParams(
            collective_id=0, has_side_effects=True, vmem_limit_bytes=63 << 20
        ),
        cost_estimate=pl.CostEstimate(
            flops=2 * ROWS * D * FQ * 6, bytes_accessed=12 << 20, transcendentals=ROWS * FQ
        ),
        name="expert_gradients",
    )(ids, probs, gain, *arrays)


def body(
    attn_input,
    kv_gain,
    latent_cot,
    attn_resid,
    moe_input,
    moe_cot,
    expert_ids,
    gate_probs,
    w_gate,
    w_up,
    w_down,
    gate_resid,
    up_resid,
    down_resid,
):
    latent_sum, terms = run_kernel(
        expert_ids.T,
        gate_probs.T,
        kv_gain[None, :],
        moe_input,
        moe_cot,
        attn_input,
        latent_cot,
        w_gate,
        w_up,
        w_down,
    )
    kv_grad = (latent_sum[:14] + attn_resid).astype(BF16)
    even = lax.rem(lax.axis_index("edp_1"), 2) == 0
    main = jnp.concatenate([terms[:, :384], terms[:, 384:768]], axis=0)
    lower, upper = terms[:, 768:832], terms[:, 832:896]
    edge = jnp.concatenate(
        [jnp.where(even, lower, upper), jnp.where(even, upper, lower)], axis=0
    )
    summed = jnp.where(
        even, jnp.concatenate([main, edge], axis=1), jnp.concatenate([edge, main], axis=1)
    )
    gate_grad = (summed[:FQ].T + gate_resid).astype(BF16)
    up_grad = (summed[FQ : 2 * FQ].T + up_resid).astype(BF16)
    down_grad = (summed[2 * FQ :] + down_resid).astype(BF16)
    return (kv_grad, gate_grad, up_grad, down_grad)


def solution(mesh):
    torus = Mesh(mesh.devices.reshape(2, 4, 4, 4, 2), ("edp_0", "edp_1", "ep_0", "ep_1", "ep_2"))
    return jax.shard_map(
        body,
        mesh=torus,
        in_specs=(
            P(EDP_EP, None),
            P(),
            P(EDP_EP, None),
            P(EDP_EP, None),
            P(EDP_EP, None),
            P(EDP_EP, None),
            P(EDP_EP, None),
            P(EDP_EP, None),
            P(None, EP),
            P(None, EP),
            P(EP, None),
            P(EDP, EP),
            P(EDP, EP),
            P(EP, EDP),
        ),
        out_specs=(P(EDP_EP, None), P(EDP, EP), P(EDP, EP), P(EP, EDP)),
        check_vma=False,
    )
```

```python
import jax
import jax.numpy as jnp
from jax import lax
from jax.experimental import pallas as pl
from jax.experimental.pallas import tpu as pltpu
from jax.sharding import Mesh
from jax.sharding import PartitionSpec as P

MESH = pl.DeviceIdType.MESH
EDP_EP = ("edp_0", "edp_1", "ep_0", "ep_1", "ep_2")
EP = ("ep_0", "ep_1", "ep_2")
EDP = ("edp_0", "edp_1")
F32, BF16 = jnp.float32, jnp.bfloat16

epsilon = 1e-06

D, TOK, FQ, CAP, KVL = 3584, 128, 256, 40, 512
EXPERTS = 8
BLOCK = 2 * CAP
CHUNK = 4 * BLOCK
ROWS = 4 * CHUNK
PIECES = 4
WIDE = D // PIECES
PAIR = 896
SLICE = 2688
EARLY = 1536
LATE = SLICE - EARLY
TURN = LATE // 2
COPIES = 136


def kernel(
    ids_ref,
    probs_ref,
    gain_ref,
    input_hbm,
    cot_hbm,
    attn_hbm,
    latent_hbm,
    w_gate_hbm,
    w_up_hbm,
    w_down_hbm,
    kv_out,
    sums_out,
    own,
    tokens,
    meta,
    ready,
    passing,
    rows,
    w_gate_up,
    w_down,
    latent,
    hidden_t,
    work,
    parts,
    early_first,
    early_sums,
    early_zl,
    late_zl,
    late_first,
    late_sums,
    kv_core,
    kv_x,
    kv_x_sum,
    kv_y,
    kv_y_sum,
    kv_z,
    send_sems,
    recv_sems,
    load_sems,
):
    zl, x, y = lax.axis_index("edp_0"), lax.axis_index("edp_1"), lax.axis_index("ep_0")
    zh, c = lax.axis_index("ep_1"), lax.axis_index("ep_2")
    z = zh * 2 + zl
    other = 1 - c

    def at_z(target):
        return (lax.rem(target, 2), x, y, target // 2, c)

    def at_y(target):
        return (zl, x, target, zh, c)

    def at_x(target):
        return (zl, target, y, zh, c)

    other_core = (zl, x, y, zh, other)
    other_zl = (1 - zl, x, y, zh, c)

    used = [0]

    def remote(src, dst, device, index=None):
        if index is None:
            index = used[0]
            used[0] += 1
        return pltpu.make_async_remote_copy(
            src_ref=src,
            dst_ref=dst,
            send_sem=send_sems.at[index],
            recv_sem=recv_sems.at[index],
            device_id=device,
            device_id_type=MESH,
        )

    loads = [0]

    def local(src, dst):
        copy = pltpu.make_async_copy(src, dst, load_sems.at[loads[0]])
        loads[0] += 1
        return copy

    load_own = [local(input_hbm, own.at[0]), local(cot_hbm, own.at[1])]
    load_later = [
        local(w_gate_hbm, w_gate_up.at[:, pl.ds(0, FQ)]),
        local(w_up_hbm, w_gate_up.at[:, pl.ds(FQ, FQ)]),
        local(w_down_hbm, w_down),
    ]
    load_latent = local(latent_hbm, latent)
    for copy in load_own + load_later + [load_latent]:
        copy.start()

    barrier = pltpu.get_barrier_semaphore()
    partners = [other_core]
    partners += [at_z(lax.rem(z + step, 8)) for step in range(1, 8)]
    partners += [at_y(lax.rem(y + step, 4)) for step in range(1, 4)]
    partners += [at_x(lax.rem(x + step, 4)) for step in range(1, 4)]
    for partner in partners:
        pl.semaphore_signal(barrier, inc=1, device_id=partner, device_id_type=MESH)

    expert = lax.broadcasted_iota(jnp.int32, (EXPERTS, TOK), 0)
    first, second = ids_ref[0:1, :] == expert, ids_ref[1:2, :] == expert
    chosen = jnp.where(first | second, 1.0, 0.0)
    earlier = lax.broadcasted_iota(jnp.int32, (TOK, TOK), 0) < lax.broadcasted_iota(
        jnp.int32, (TOK, TOK), 1
    )
    position = jnp.dot(
        chosen.astype(BF16),
        jnp.where(earlier, 1.0, 0.0).astype(BF16),
        preferred_element_type=F32,
    )
    shift = (c * CAP).astype(F32)
    meta[0, c, 0:8, :] = jnp.where(first | second, position + shift, -1.0)
    meta[0, c, 8:16, :] = jnp.where(first, probs_ref[0:1, :], 0.0) + jnp.where(
        second, probs_ref[1:2, :], 0.0
    )

    pl.semaphore_wait(barrier, len(partners))

    mine = pl.ds(pl.multiple_of(c * TOK, TOK), TOK)
    theirs = pl.ds(pl.multiple_of(other * TOK, TOK), TOK)
    for copy in load_own:
        copy.wait()
    swap = remote(own.at[other], tokens.at[0, mine], other_core)
    swap.start()
    swap_in = remote(own.at[other], tokens.at[0, theirs], other_core, used[0] - 1)
    swap_meta = remote(meta.at[0, c], meta.at[0, c], other_core)
    swap_meta.start()
    swap_meta_in = remote(meta.at[0, other], meta.at[0, other], other_core, used[0] - 1)
    keep = local(own.at[c], tokens.at[0, mine])
    keep.start()
    swap_meta_in.wait_recv()
    swap_in.wait_recv()
    keep.wait()

    even = 1 - lax.rem(z, 2)
    near = lax.rem(z + 9 - 2 * even, 8)
    far = lax.rem(z + 4 * even + 6, 8)
    columns = [pl.ds(piece * WIDE, WIDE) for piece in range(PIECES)]

    def along_z(source, slot, target):
        return [remote(meta.at[source], meta.at[slot], at_z(target))] + [
            remote(tokens.at[source, :, part], tokens.at[slot, :, part], at_z(target))
            for part in columns
        ]

    z_near, z_far = along_z(0, 1, near), along_z(0, 2, far)
    z_next = along_z(1, 3, far)
    for copy in z_near:
        copy.start()

    half = zh // 2
    up, down = lax.rem(y + 1, 4), lax.rem(y + 3, 4)
    onward = lax.rem(y + 1 + 2 * c, 4)
    slot_of = lax.broadcasted_iota(jnp.int32, (BLOCK, TOK), 0).astype(F32)
    core_weight = c.astype(F32)

    def block_rows(chunk, step):
        return pl.ds(chunk * CHUNK + step * BLOCK, BLOCK)

    y_sent, y_passed, core_sent, core_got = {}, {}, {}, {}
    for chunk in range(4):
        for piece in range(PIECES):
            part, slot = columns[piece], chunk % 2
            y_sent[chunk, piece] = [
                remote(
                    ready.at[slot, 0, :, part],
                    rows.at[c, block_rows(chunk, 1), part],
                    at_y(up),
                ),
                remote(ready.at[slot, 1, :, part], passing.at[chunk, :, part], at_y(onward)),
                remote(
                    ready.at[slot, 2, :, part],
                    rows.at[c, block_rows(chunk, 3), part],
                    at_y(down),
                ),
            ]
            y_passed[chunk, piece] = remote(
                passing.at[chunk, :, part],
                rows.at[c, block_rows(chunk, 2), part],
                at_y(onward),
            )
            whole = pl.ds(chunk * CHUNK, CHUNK)
            core_sent[chunk, piece] = remote(
                rows.at[c, whole, part], rows.at[c, whole, part], other_core
            )
            core_got[chunk, piece] = remote(
                rows.at[other, whole, part], rows.at[other, whole, part], other_core, used[0] - 1
            )

    def send_rows(chunk, piece):
        part = columns[piece]
        for step in (2, 1, 3, 0):
            name = lax.rem(y + step, 4) * 2 + half
            hot = [
                meta[chunk, core, pl.ds(name, 1), :] == slot_of for core in range(2)
            ]
            hot = [jnp.where(one, 1.0, 0.0) for one in hot]
            weight = sum(
                jnp.sum(one * meta[chunk, core, pl.ds(name + 8, 1), :], axis=1, keepdims=True)
                for core, one in enumerate(hot)
            )
            scale = weight * core_weight + (1.0 - core_weight)
            picked = jnp.dot(
                jnp.concatenate(hot, axis=1).astype(BF16),
                tokens[chunk, :, part],
                preferred_element_type=F32,
            )
            picked = (picked * scale).astype(BF16)
            if step == 0:
                rows[c, block_rows(chunk, 0), part] = picked
            else:
                if chunk >= 2:
                    y_sent[chunk - 2, piece][step - 1].wait_send()
                ready[chunk % 2, step - 1, :, part] = picked
                y_sent[chunk, piece][step - 1].start()

    def pass_rows(chunk, piece):
        y_sent[chunk, piece][1].wait_recv()
        y_passed[chunk, piece].start()

    def share_rows(chunk, piece):
        y_sent[chunk, piece][0].wait_recv()
        y_sent[chunk, piece][2].wait_recv()
        y_passed[chunk, piece].wait_recv()
        core_sent[chunk, piece].start()

    for piece in range(PIECES):
        send_rows(0, piece)

    swap.wait_send()
    load_attn = local(attn_hbm, own.at[0])
    load_attn.start()
    load_latent.wait()
    load_attn.wait()

    @pl.loop(0, TOK // 16)
    def _(tile):
        part = pl.ds(pl.multiple_of(tile * 16, 16), 16)
        values = own[0, part, :].astype(F32)
        inv_rms = lax.rsqrt(jnp.mean(values * values, axis=1, keepdims=True) + epsilon)
        own[1, part, :] = (values * inv_rms * gain_ref[...]).astype(BF16)

    work[896:904, 0:KVL] = jnp.zeros((8, KVL), F32)

    @pl.loop(0, 4)
    def _(tile):
        normed = own[1, :, pl.ds(pl.multiple_of(tile * PAIR, 128), PAIR)]
        work[0:896, 0:KVL] = lax.dot_general(
            normed, latent[...], (((0,), (0,)), ((), ())), preferred_element_type=F32
        )
        start = lax.rem(tile, 2) * 4096 + (tile // 2) * 64
        for place in range(64):
            fixed = (place % 2) * 8192 + (place // 8) * 512 + (place % 8 // 2) * 128
            share = work[14 * place : 14 * place + 16, 0:KVL].astype(BF16)
            for lane in range(4):
                to = pl.multiple_of(start + fixed + lane * 16, 16)
                parts[pl.ds(to, 16), :] = share[:, lane * 128 : lane * 128 + 128]

    def half_of(core):
        return pl.multiple_of(core * 8192, 8192)

    kv_to_core = remote(parts.at[pl.ds(half_of(other), 8192)], kv_core, other_core)
    kv_to_core.start()

    for piece in range(PIECES):
        pass_rows(0, piece)

    kv_to_core.wait_recv()

    @pl.loop(0, 16)
    def _(tile):
        at = pl.multiple_of(tile * 512, 512)
        here = pl.ds(half_of(c) + at, 512)
        parts[here, :] = (
            parts[here, :].astype(F32) + kv_core[pl.ds(at, 512), :].astype(F32)
        ).astype(BF16)

    kv_to_x = []
    for step in range(1, 4):
        target = lax.rem(x + step, 4)
        at = pl.ds(half_of(c) + pl.multiple_of(target * 2048, 2048), 2048)
        kv_to_x.append(remote(parts.at[at], kv_x.at[step - 1], at_x(target)))
        kv_to_x[-1].start()

    for piece in range(PIECES):
        share_rows(0, piece)

    z_near[0].wait_recv()
    for piece in range(PIECES):
        z_near[1 + piece].wait_recv()
        if piece == PIECES - 2:
            z_far[0].start()
            z_far[1].start()
        if piece == PIECES - 1:
            for copy in z_far[2:]:
                copy.start()
        send_rows(1, piece)

    for copy in kv_to_x:
        copy.wait()

    @pl.loop(0, 4)
    def _(tile):
        at = pl.multiple_of(tile * 512, 512)
        total = parts[pl.ds(half_of(c) + pl.multiple_of(x * 2048, 2048) + at, 512), :].astype(F32)
        for step in range(3):
            total = total + kv_x[step, pl.ds(at, 512), :].astype(F32)
        kv_x_sum[pl.ds(at, 512), :] = total.astype(BF16)

    kv_to_y = []
    for step in range(1, 4):
        target = lax.rem(y + step, 4)
        at = pl.ds(pl.multiple_of(target * 512, 512), 512)
        kv_to_y.append(remote(kv_x_sum.at[at], kv_y.at[step - 1], at_y(target)))
        kv_to_y[-1].start()

    for piece in range(PIECES):
        pass_rows(1, piece)
    for piece in range(PIECES):
        share_rows(1, piece)

    for copy in kv_to_y:
        copy.wait()
    total = kv_x_sum[pl.ds(pl.multiple_of(y * 512, 512), 512), :].astype(F32)
    for step in range(3):
        total = total + kv_y[step].astype(F32)
    kv_y_sum[...] = total.astype(BF16)
    kv_to_z = []
    for step in range(1, 8):
        target = lax.rem(z + step, 8)
        at = pl.ds(pl.multiple_of(target * 64, 64), 64)
        kv_to_z.append(remote(kv_y_sum.at[at], kv_z.at[step - 1], at_z(target)))
        kv_to_z[-1].start()

    z_far[0].wait_recv()
    for piece in range(PIECES):
        z_far[1 + piece].wait_recv()
        if piece == PIECES - 2:
            for copy in z_next[:3]:
                copy.start()
        if piece == PIECES - 1:
            for copy in z_next[3:]:
                copy.start()
        send_rows(2, piece)
        if piece:
            pass_rows(2, piece - 1)

    def hidden_units(start, tall, chunks):
        for chunk in chunks:
            for piece in range(PIECES):
                core_got[chunk, piece].wait_recv()
        group = pl.ds(start, tall)
        work[0:tall, 0 : 3 * FQ] = jnp.zeros((tall, 3 * FQ), F32)

        @pl.loop(0, 7)
        def _(tile):
            at = pl.ds(pl.multiple_of(tile * 512, 512), 512)
            work[0:tall, 0 : 2 * FQ] += jnp.dot(
                rows[0, group, at], w_gate_up[at, :], preferred_element_type=F32
            )
            work[0:tall, 2 * FQ : 3 * FQ] += lax.dot_general(
                rows[1, group, at],
                w_down[:, at],
                (((1,), (1,)), ((), ())),
                preferred_element_type=F32,
            )

        @pl.loop(0, tall // 128)
        def _(tile):
            at = pl.ds(pl.multiple_of(tile * 128, 128), 128)
            to = pl.ds(pl.multiple_of(start + tile * 128, 128), 128)
            gate, up_proj = work[at, 0:FQ], work[at, FQ : 2 * FQ]
            back = work[at, 2 * FQ : 3 * FQ]
            sigmoid = jax.nn.sigmoid(gate)
            active = gate * sigmoid * up_proj
            up_rows = back * gate * sigmoid
            gate_rows = back * up_proj * sigmoid * (1.0 + gate * (1.0 - sigmoid))
            hidden_t[0:FQ, to] = gate_rows.T.astype(BF16)
            hidden_t[FQ : 2 * FQ, to] = up_rows.T.astype(BF16)
            hidden_t[2 * FQ : 3 * FQ, to] = active.T.astype(BF16)

    for copy in load_later:
        copy.wait()
    hidden_units(0, 2 * CHUNK, (0, 1))

    pass_rows(2, PIECES - 1)
    for piece in range(PIECES):
        share_rows(2, piece)

    for copy in kv_to_z:
        copy.wait()
    total = kv_y_sum[pl.ds(pl.multiple_of(z * 64, 64), 64), :].astype(F32)
    for step in range(7):
        total = total + kv_z[step].astype(F32)
    for lane in range(4):
        kv_out[:, lane * 128 : lane * 128 + 128] = total[lane * 16 : lane * 16 + 16, :]
    kv_to_core.wait_send()

    z_next[0].wait_recv()
    for piece in range(PIECES):
        z_next[1 + piece].wait_recv()
        send_rows(3, piece)
        if piece:
            pass_rows(3, piece - 1)
    pass_rows(3, PIECES - 1)
    hidden_units(2 * CHUNK, 256, (2,))
    for piece in range(PIECES):
        share_rows(3, piece)
    hidden_units(2 * CHUNK + 256, 2 * CHUNK - 256, (3,))

    across, far_half = lax.rem(x + 2, 4), 1 - zl
    side = x // 2
    turns = [lax.rem(x + 1, 4), lax.rem(x + 3, 4)]

    def early(which):
        return pl.ds(pl.multiple_of(which * SLICE, 128), EARLY)

    def late(which, turn=None):
        at = which * SLICE + EARLY
        if turn is None:
            return pl.ds(pl.multiple_of(at, 128), LATE)
        return pl.ds(pl.multiple_of(at + turn * TURN, 64), TURN)

    low = lax.broadcasted_iota(jnp.int32, (384, 128), 1) < 64

    def gradients(pair):
        at = pl.ds(pl.multiple_of(pair * PAIR, 128), PAIR)
        work[0 : 2 * FQ, :] = jnp.dot(
            hidden_t[0 : 2 * FQ, :], rows[0, :, at], preferred_element_type=F32
        )
        work[2 * FQ : 3 * FQ, :] = jnp.dot(
            hidden_t[2 * FQ : 3 * FQ, :], rows[1, :, at], preferred_element_type=F32
        )
        start = pair * 2 * SLICE

        def put(which, block, value):
            to = pl.multiple_of(start + which * SLICE + block * 384, 128)
            parts[pl.ds(to, 384), :] = value.astype(BF16)

        for lane in range(3):
            for tall in range(2):
                high = slice(tall * 384, tall * 384 + 384)
                put(0, tall * 3 + lane, work[high, lane * 128 : lane * 128 + 128])
                put(1, tall * 3 + lane, work[high, 512 + lane * 128 : 640 + lane * 128])
        top, bottom = work[0:384, 384:512], pltpu.roll(work[384:768, 384:512], 64, 1)
        put(0, 6, jnp.where(low, top, bottom))
        put(1, 6, jnp.where(low, bottom, top))

    def onward_x(half):
        return lax.rem(x + 1 + 2 * half, 4)

    def back_x(half):
        return lax.rem(x + 3 + 2 * half, 4)

    def add_rows(start, count, tile_rows, *added):
        @pl.loop(0, count // tile_rows)
        def _(tile):
            at = pl.multiple_of(tile * tile_rows, 64)
            here = pl.ds(pl.multiple_of(start + at, 64), tile_rows)
            total = parts[here, :].astype(F32)
            for one in added:
                total = total + one[pl.ds(at, tile_rows), :].astype(F32)
            parts[here, :] = total.astype(BF16)

    sums_sent = []

    def send(src, dst, device):
        copy = remote(src, dst, device)
        copy.start()
        sums_sent.append(copy)
        return copy

    def send_zl(target):
        return send(parts.at[late(far_half * 4 + target)], late_zl.at[target], other_zl)

    def send_across(half):
        return send(
            parts.at[early(half * 4 + across)], early_first.at[half], at_x(onward_x(half))
        )

    zl_sent = {}
    gradients(far_half * 2 + 1 - side)
    for place in range(2):
        zl_sent[place] = send_zl((1 - side) * 2 + place)
    far_across = send_across(far_half)
    gradients(zl * 2 + 1 - side)
    near_across = send_across(zl)
    gradients(far_half * 2 + side)
    for place in range(2):
        zl_sent[2 + place] = send_zl(side * 2 + place)
    gradients(zl * 2 + side)
    plain = [
        send(
            parts.at[early(half * 4 + back_x(half))],
            early_sums.at[half, 1],
            at_x(back_x(half)),
        )
        for half in (far_half, zl)
    ]
    merged = []
    for half, copy in ((far_half, far_across), (zl, near_across)):
        copy.wait_recv()
        ahead = half * 4 + onward_x(half)
        add_rows(ahead * SLICE, EARLY, 384, early_first.at[half])
        merged.append(
            send(parts.at[early(ahead)], early_sums.at[half, 0], at_x(onward_x(half)))
        )

    for copy in zl_sent.values():
        copy.wait_recv()

    def take_zl(target):
        add_rows((zl * 4 + target) * SLICE + EARLY, LATE, 384, late_zl.at[target])

    def turn_rows(turn):
        return pl.ds(turn * TURN, TURN)

    take_zl(across)
    late_across = [
        send(
            parts.at[late(zl * 4 + across, turn)], late_first.at[turn_rows(turn)], at_x(turns[turn])
        )
        for turn in range(2)
    ]
    for target in turns:
        take_zl(target)
    late_plain = [
        send(
            parts.at[late(zl * 4 + turns[1 - turn], turn)],
            late_sums.at[1, turn_rows(turn)],
            at_x(turns[1 - turn]),
        )
        for turn in range(2)
    ]
    take_zl(x)

    for copy in (plain[0], merged[0]):
        copy.wait_recv()
    here = far_half * 4 + x
    add_rows(
        here * SLICE, EARLY, 384, early_sums.at[far_half, 0], early_sums.at[far_half, 1]
    )
    early_last = send(parts.at[early(here)], early_zl, other_zl)

    late_merged = []
    for turn in range(2):
        late_across[turn].wait_recv()
        ahead = zl * 4 + turns[turn]
        add_rows(
            ahead * SLICE + EARLY + turn * TURN, TURN, 192, late_first.at[turn_rows(turn)]
        )
        late_merged.append(
            send(
                parts.at[late(ahead, turn)], late_sums.at[0, turn_rows(turn)], at_x(turns[turn])
            )
        )

    mine_at = (zl * 4 + x) * SLICE

    def put_sum(block, added):
        total = parts[pl.ds(pl.multiple_of(mine_at + block * 384, 128), 384), :].astype(F32)
        for one in added:
            total = total + one.astype(F32)
        work[0:384, block * 128 : block * 128 + 128] = total

    for copy in (plain[1], merged[1], early_last):
        copy.wait_recv()
    for block in range(4):
        at = pl.ds(block * 384, 384)
        put_sum(block, (early_sums[zl, 0, at, :], early_sums[zl, 1, at, :], early_zl[at, :]))
    for copy in late_plain + late_merged:
        copy.wait_recv()
    for block in range(3):
        at = pl.ds(block * 384, 384)
        put_sum(4 + block, (late_sums[0, at, :], late_sums[1, at, :]))

    odd = lax.rem(x, 2)
    main = pl.ds(pl.multiple_of(384 + odd * 64, 64), 384)
    edge = pl.ds(pl.multiple_of(768 - odd * 384, 64), 64)
    edges = work[0:384, 768:896].T
    swapped = lax.broadcasted_iota(jnp.int32, (64, 384), 0) * 0 + odd == 1
    work[edge, 0:384] = jnp.where(swapped, edges[64:128, :], edges[0:64, :])
    work[edge, 384:768] = jnp.where(swapped, edges[0:64, :], edges[64:128, :])
    for tall in range(2):
        high = slice(tall * 384, tall * 384 + 384)
        work[main, high] = work[0:384, high].T
    store = local(work.at[pl.ds(384, 448), pl.ds(0, 768)], sums_out)
    store.start()

    for copy in [swap_meta] + sums_sent:
        copy.wait_send()
    for group in (z_near, z_far, z_next):
        for copy in group:
            copy.wait_send()
    for chunk in range(4):
        for piece in range(PIECES):
            if chunk >= 2:
                for copy in y_sent[chunk, piece]:
                    copy.wait_send()
            y_passed[chunk, piece].wait_send()
            core_sent[chunk, piece].wait_send()
    store.wait()


def run_kernel(ids, probs, gain, *arrays):
    vmem, any_space = pl.BlockSpec(memory_space=pltpu.VMEM), pl.BlockSpec(memory_space=pl.ANY)
    return pl.pallas_call(
        kernel,
        out_shape=(
            jax.ShapeDtypeStruct((16, KVL), F32),
            jax.ShapeDtypeStruct((448, 3 * FQ), F32),
        ),
        in_specs=[vmem] * 3 + [any_space] * len(arrays),
        out_specs=(vmem, any_space),
        scratch_shapes=[
            pltpu.VMEM((2, TOK, D), BF16),
            pltpu.VMEM((4, 2 * TOK, D), BF16),
            pltpu.VMEM((4, 2, 16, TOK), F32),
            pltpu.VMEM((2, 3, BLOCK, D), BF16),
            pltpu.VMEM((4, BLOCK, D), BF16),
            pltpu.VMEM((2, ROWS, D), BF16),
            pltpu.VMEM((D, 2 * FQ), BF16),
            pltpu.VMEM((FQ, D), BF16),
            pltpu.VMEM((TOK, KVL), BF16),
            pltpu.VMEM((3 * FQ, ROWS), BF16),
            pltpu.VMEM((904, PAIR), F32),
            pltpu.VMEM((8 * SLICE, 128), BF16),
            pltpu.VMEM((2, EARLY, 128), BF16),
            pltpu.VMEM((2, 2, EARLY, 128), BF16),
            pltpu.VMEM((EARLY, 128), BF16),
            pltpu.VMEM((4, LATE, 128), BF16),
            pltpu.VMEM((LATE, 128), BF16),
            pltpu.VMEM((2, LATE, 128), BF16),
            pltpu.VMEM((8192, 128), BF16),
            pltpu.VMEM((3, 2048, 128), BF16),
            pltpu.VMEM((2048, 128), BF16),
            pltpu.VMEM((3, 512, 128), BF16),
            pltpu.VMEM((512, 128), BF16),
            pltpu.VMEM((7, 64, 128), BF16),
            pltpu.SemaphoreType.DMA((COPIES,)),
            pltpu.SemaphoreType.DMA((COPIES,)),
            pltpu.SemaphoreType.DMA((12,)),
        ],
        compiler_params=pltpu.CompilerParams(
            collective_id=0, has_side_effects=True, vmem_limit_bytes=63 << 20
        ),
        cost_estimate=pl.CostEstimate(
            flops=2 * ROWS * D * FQ * 6, bytes_accessed=12 << 20, transcendentals=ROWS * FQ
        ),
        name="expert_gradients",
    )(ids, probs, gain, *arrays)


def body(
    attn_input,
    kv_gain,
    latent_cot,
    attn_resid,
    moe_input,
    moe_cot,
    expert_ids,
    gate_probs,
    w_gate,
    w_up,
    w_down,
    gate_resid,
    up_resid,
    down_resid,
):
    latent_sum, sums = run_kernel(
        expert_ids.T,
        gate_probs.T,
        kv_gain[None, :],
        moe_input,
        moe_cot,
        attn_input,
        latent_cot,
        w_gate,
        w_up,
        w_down,
    )
    kv_grad = (latent_sum[:14] + attn_resid).astype(BF16)
    gate_grad = (sums[:, :FQ] + gate_resid).astype(BF16)
    up_grad = (sums[:, FQ : 2 * FQ] + up_resid).astype(BF16)
    down_grad = (sums[:, 2 * FQ :] + down_resid.T).astype(BF16).T
    return (kv_grad, gate_grad, up_grad, down_grad)


def solution(mesh):
    torus = Mesh(mesh.devices.reshape(2, 4, 4, 4, 2), ("edp_0", "edp_1", "ep_0", "ep_1", "ep_2"))
    return jax.shard_map(
        body,
        mesh=torus,
        in_specs=(
            P(EDP_EP, None),
            P(),
            P(EDP_EP, None),
            P(EDP_EP, None),
            P(EDP_EP, None),
            P(EDP_EP, None),
            P(EDP_EP, None),
            P(EDP_EP, None),
            P(None, EP),
            P(None, EP),
            P(EP, None),
            P(EDP, EP),
            P(EDP, EP),
            P(EP, EDP),
        ),
        out_specs=(P(EDP_EP, None), P(EDP, EP), P(EDP, EP), P(EP, EDP)),
        check_vma=False,
    )
```

```python
import jax
import jax.numpy as jnp
from jax import lax
from jax.experimental import pallas as pl
from jax.experimental.pallas import tpu as pltpu
from jax.sharding import Mesh
from jax.sharding import PartitionSpec as P

MESH = pl.DeviceIdType.MESH
EDP_EP = ("edp_0", "edp_1", "ep_0", "ep_1", "ep_2")
EP = ("ep_0", "ep_1", "ep_2")
EDP = ("edp_0", "edp_1")
F32, BF16 = jnp.float32, jnp.bfloat16

epsilon = 1e-06

D, TOK, FQ, CAP, KVL = 3584, 128, 256, 40, 512
EXPERTS = 8
BLOCK = 2 * CAP
CHUNK = 4 * BLOCK
ROWS = 4 * CHUNK
PIECES = 4
BOUNDS = (0, 896, 1792, 2688, D)
TILE = 896
PAIR = 896
SLICE = 2688
EARLY = 1536
LATE = SLICE - EARLY
TURN = LATE // 2
COPIES = 144


def kernel(
    ids_ref,
    probs_ref,
    gain_hbm,
    input_hbm,
    cot_hbm,
    attn_hbm,
    latent_hbm,
    w_gate_hbm,
    w_up_hbm,
    w_down_hbm,
    kv_out,
    sums_out,
    own,
    tokens,
    meta,
    ready,
    passing,
    rows,
    w_gate_up,
    w_down,
    latent,
    gain,
    hidden_t,
    work,
    parts,
    early_first,
    early_sums,
    early_zl,
    late_zl,
    late_first,
    late_sums,
    kv_core,
    kv_x,
    kv_x_sum,
    kv_y,
    kv_y_sum,
    kv_z,
    send_sems,
    recv_sems,
    load_sems,
):
    zl, x, y = lax.axis_index("edp_0"), lax.axis_index("edp_1"), lax.axis_index("ep_0")
    zh, c = lax.axis_index("ep_1"), lax.axis_index("ep_2")
    z = zh * 2 + zl
    other = 1 - c

    def at_z(target):
        return (lax.rem(target, 2), x, y, target // 2, c)

    def at_y(target):
        return (zl, x, target, zh, c)

    def at_x(target):
        return (zl, target, y, zh, c)

    other_core = (zl, x, y, zh, other)
    other_zl = (1 - zl, x, y, zh, c)

    used = [0]

    def remote(src, dst, device, index=None):
        if index is None:
            index = used[0]
            used[0] += 1
        return pltpu.make_async_remote_copy(
            src_ref=src,
            dst_ref=dst,
            send_sem=send_sems.at[index],
            recv_sem=recv_sems.at[index],
            device_id=device,
            device_id_type=MESH,
        )

    loads = [0]

    def local(src, dst):
        copy = pltpu.make_async_copy(src, dst, load_sems.at[loads[0]])
        loads[0] += 1
        return copy

    load_own = [local(input_hbm, own.at[0]), local(cot_hbm, own.at[1])]
    load_later = [
        local(w_gate_hbm, w_gate_up.at[:, pl.ds(0, FQ)]),
        local(w_up_hbm, w_gate_up.at[:, pl.ds(FQ, FQ)]),
        local(w_down_hbm, w_down),
    ]
    load_latent = [local(latent_hbm, latent), local(gain_hbm, gain.at[0])]
    for copy in load_own + load_later + load_latent:
        copy.start()

    barrier = pltpu.get_barrier_semaphore()
    partners = [other_core]
    partners += [at_z(lax.rem(z + step, 8)) for step in range(1, 8)]
    partners += [at_y(lax.rem(y + step, 4)) for step in range(1, 4)]
    partners += [at_x(lax.rem(x + step, 4)) for step in range(1, 4)]
    for partner in partners:
        pl.semaphore_signal(barrier, inc=1, device_id=partner, device_id_type=MESH)

    expert = lax.broadcasted_iota(jnp.int32, (EXPERTS, TOK), 0)
    first, second = ids_ref[0:1, :] == expert, ids_ref[1:2, :] == expert
    chosen = jnp.where(first | second, 1.0, 0.0)
    earlier = lax.broadcasted_iota(jnp.int32, (TOK, TOK), 0) < lax.broadcasted_iota(
        jnp.int32, (TOK, TOK), 1
    )
    position = jnp.dot(
        chosen.astype(BF16),
        jnp.where(earlier, 1.0, 0.0).astype(BF16),
        preferred_element_type=F32,
    )
    shift = (c * CAP).astype(F32)
    meta[0, c, 0:8, :] = jnp.where(first | second, position + shift, -1.0)
    meta[0, c, 8:16, :] = jnp.where(first, probs_ref[0:1, :], 0.0) + jnp.where(
        second, probs_ref[1:2, :], 0.0
    )

    pl.semaphore_wait(barrier, len(partners))

    mine = pl.ds(pl.multiple_of(c * TOK, TOK), TOK)
    theirs = pl.ds(pl.multiple_of(other * TOK, TOK), TOK)
    columns = [pl.ds(at, to - at) for at, to in zip(BOUNDS, BOUNDS[1:])]

    even = 1 - lax.rem(z, 2)
    near = lax.rem(z + 9 - 2 * even, 8)
    far = lax.rem(z + 4 * even + 6, 8)

    for copy in load_own:
        copy.wait()
    swap_meta = remote(meta.at[0, c], meta.at[0, c], other_core)
    swap_meta.start()
    swap_meta_in = remote(meta.at[0, other], meta.at[0, other], other_core, used[0] - 1)
    swap = remote(own.at[other], tokens.at[0, mine], other_core)
    swap.start()
    swap_in = remote(own.at[other], tokens.at[0, theirs], other_core, used[0] - 1)
    keep = local(own.at[c], tokens.at[0, mine])
    keep.start()
    swap_meta_in.wait_recv()
    swap_in.wait_recv()
    keep.wait()

    def along_z(source, slot, target):
        return [remote(meta.at[source], meta.at[slot], at_z(target))] + [
            remote(tokens.at[source, :, part], tokens.at[slot, :, part], at_z(target))
            for part in columns
        ]

    z_near, z_far, z_next = along_z(0, 1, near), along_z(0, 2, far), along_z(1, 3, far)
    for copy in z_near:
        copy.start()

    half = zh // 2
    up, down = lax.rem(y + 1, 4), lax.rem(y + 3, 4)
    onward = lax.rem(y + 1 + 2 * c, 4)
    slot_of = lax.broadcasted_iota(jnp.int32, (BLOCK, TOK), 0).astype(F32)
    core_weight = c.astype(F32)

    def block_rows(chunk, step):
        return pl.ds(chunk * CHUNK + step * BLOCK, BLOCK)

    y_sent, y_passed, core_sent, core_got = {}, {}, {}, {}
    for chunk in range(4):
        for piece in range(PIECES):
            part, slot = columns[piece], chunk % 2
            y_sent[chunk, piece] = [
                remote(
                    ready.at[slot, 0, :, part],
                    rows.at[c, block_rows(chunk, 1), part],
                    at_y(up),
                ),
                remote(ready.at[slot, 1, :, part], passing.at[chunk, :, part], at_y(onward)),
                remote(
                    ready.at[slot, 2, :, part],
                    rows.at[c, block_rows(chunk, 3), part],
                    at_y(down),
                ),
            ]
            y_passed[chunk, piece] = remote(
                passing.at[chunk, :, part],
                rows.at[c, block_rows(chunk, 2), part],
                at_y(onward),
            )
            whole = pl.ds(chunk * CHUNK, CHUNK)
            core_sent[chunk, piece] = remote(
                rows.at[c, whole, part], rows.at[c, whole, part], other_core
            )
            core_got[chunk, piece] = remote(
                rows.at[other, whole, part], rows.at[other, whole, part], other_core, used[0] - 1
            )

    def send_rows(chunk, piece):
        part = columns[piece]
        for step in (2, 1, 3, 0):
            name = lax.rem(y + step, 4) * 2 + half
            hot = [
                meta[chunk, core, pl.ds(name, 1), :] == slot_of for core in range(2)
            ]
            hot = [jnp.where(one, 1.0, 0.0) for one in hot]
            weight = sum(
                jnp.sum(one * meta[chunk, core, pl.ds(name + 8, 1), :], axis=1, keepdims=True)
                for core, one in enumerate(hot)
            )
            scale = weight * core_weight + (1.0 - core_weight)
            picked = jnp.dot(
                jnp.concatenate(hot, axis=1).astype(BF16),
                tokens[chunk, :, part],
                preferred_element_type=F32,
            )
            picked = (picked * scale).astype(BF16)
            if step == 0:
                rows[c, block_rows(chunk, 0), part] = picked
            else:
                if chunk >= 2:
                    y_sent[chunk - 2, piece][step - 1].wait_send()
                ready[chunk % 2, step - 1, :, part] = picked
                y_sent[chunk, piece][step - 1].start()

    def pass_rows(chunk, piece):
        y_sent[chunk, piece][1].wait_recv()
        y_passed[chunk, piece].start()

    def share_rows(chunk, piece):
        y_sent[chunk, piece][0].wait_recv()
        y_sent[chunk, piece][2].wait_recv()
        y_passed[chunk, piece].wait_recv()
        core_sent[chunk, piece].start()

    for piece in range(PIECES):
        send_rows(0, piece)

    swap.wait_send()
    load_attn = local(attn_hbm, own.at[0])
    load_attn.start()
    for copy in load_latent:
        copy.wait()
    load_attn.wait()

    @pl.loop(0, TOK // 16)
    def _(tile):
        part = pl.ds(pl.multiple_of(tile * 16, 16), 16)
        values = own[0, part, :].astype(F32)
        inv_rms = lax.rsqrt(jnp.mean(values * values, axis=1, keepdims=True) + epsilon)
        own[1, part, :] = (values * inv_rms * gain[...]).astype(BF16)

    work[896:904, 0:KVL] = jnp.zeros((8, KVL), F32)

    @pl.loop(0, 4)
    def _(tile):
        normed = own[1, :, pl.ds(pl.multiple_of(tile * PAIR, 128), PAIR)]
        work[0:896, 0:KVL] = lax.dot_general(
            normed, latent[...], (((0,), (0,)), ((), ())), preferred_element_type=F32
        )
        start = lax.rem(tile, 2) * 4096 + (tile // 2) * 64
        for place in range(64):
            fixed = (place % 2) * 8192 + (place // 8) * 512 + (place % 8 // 2) * 128
            share = work[14 * place : 14 * place + 16, 0:KVL].astype(BF16)
            for lane in range(4):
                to = pl.multiple_of(start + fixed + lane * 16, 16)
                parts[pl.ds(to, 16), :] = share[:, lane * 128 : lane * 128 + 128]

    def half_of(core):
        return pl.multiple_of(core * 8192, 8192)

    kv_to_core = remote(parts.at[pl.ds(half_of(other), 8192)], kv_core, other_core)
    kv_to_core.start()

    for piece in range(PIECES):
        pass_rows(0, piece)

    kv_to_core.wait_recv()

    @pl.loop(0, 16)
    def _(tile):
        at = pl.multiple_of(tile * 512, 512)
        here = pl.ds(half_of(c) + at, 512)
        parts[here, :] = (
            parts[here, :].astype(F32) + kv_core[pl.ds(at, 512), :].astype(F32)
        ).astype(BF16)

    kv_to_x = []
    for step in range(1, 4):
        target = lax.rem(x + step, 4)
        at = pl.ds(half_of(c) + pl.multiple_of(target * 2048, 2048), 2048)
        kv_to_x.append(remote(parts.at[at], kv_x.at[step - 1], at_x(target)))
        kv_to_x[-1].start()

    for piece in range(PIECES):
        share_rows(0, piece)

    z_near[0].wait_recv()
    for piece in range(PIECES):
        z_near[1 + piece].wait_recv()
        if piece == PIECES - 2:
            z_far[0].start()
            z_far[1].start()
        if piece == PIECES - 1:
            for copy in z_far[2:]:
                copy.start()
        send_rows(1, piece)

    for copy in kv_to_x:
        copy.wait()

    @pl.loop(0, 4)
    def _(tile):
        at = pl.multiple_of(tile * 512, 512)
        total = parts[pl.ds(half_of(c) + pl.multiple_of(x * 2048, 2048) + at, 512), :].astype(F32)
        for step in range(3):
            total = total + kv_x[step, pl.ds(at, 512), :].astype(F32)
        kv_x_sum[pl.ds(at, 512), :] = total.astype(BF16)

    kv_to_y = []
    for step in range(1, 4):
        target = lax.rem(y + step, 4)
        at = pl.ds(pl.multiple_of(target * 512, 512), 512)
        kv_to_y.append(remote(kv_x_sum.at[at], kv_y.at[step - 1], at_y(target)))
        kv_to_y[-1].start()

    for piece in range(PIECES):
        pass_rows(1, piece)
    for piece in range(PIECES):
        share_rows(1, piece)

    for copy in kv_to_y:
        copy.wait()
    total = kv_x_sum[pl.ds(pl.multiple_of(y * 512, 512), 512), :].astype(F32)
    for step in range(3):
        total = total + kv_y[step].astype(F32)
    kv_y_sum[...] = total.astype(BF16)
    kv_to_z = []
    for step in range(1, 8):
        target = lax.rem(z + step, 8)
        at = pl.ds(pl.multiple_of(target * 64, 64), 64)
        kv_to_z.append(remote(kv_y_sum.at[at], kv_z.at[step - 1], at_z(target)))
        kv_to_z[-1].start()

    z_far[0].wait_recv()
    for piece in range(PIECES):
        z_far[1 + piece].wait_recv()
        if piece == PIECES - 2:
            for copy in z_next[:3]:
                copy.start()
        if piece == PIECES - 1:
            for copy in z_next[3:]:
                copy.start()
        send_rows(2, piece)
        if piece:
            pass_rows(2, piece - 1)

    def hidden_piece(start, tall, chunks, piece):
        for chunk in chunks:
            core_got[chunk, piece].wait_recv()
        group = pl.ds(start, tall)
        if piece == 0:
            work[0:tall, 0 : 3 * FQ] = jnp.zeros((tall, 3 * FQ), F32)

        @pl.loop(BOUNDS[piece] // TILE, BOUNDS[piece + 1] // TILE)
        def _(tile):
            at = pl.ds(pl.multiple_of(tile * TILE, TILE), TILE)
            work[0:tall, 0 : 2 * FQ] += jnp.dot(
                rows[0, group, at], w_gate_up[at, :], preferred_element_type=F32
            )
            work[0:tall, 2 * FQ : 3 * FQ] += lax.dot_general(
                rows[1, group, at],
                w_down[:, at],
                (((1,), (1,)), ((), ())),
                preferred_element_type=F32,
            )

    def hidden_end(start, tall):
        @pl.loop(0, tall // 128)
        def _(tile):
            at = pl.ds(pl.multiple_of(tile * 128, 128), 128)
            to = pl.ds(pl.multiple_of(start + tile * 128, 128), 128)
            gate, up_proj = work[at, 0:FQ], work[at, FQ : 2 * FQ]
            back = work[at, 2 * FQ : 3 * FQ]
            sigmoid = jax.nn.sigmoid(gate)
            active = gate * sigmoid * up_proj
            up_rows = back * gate * sigmoid
            gate_rows = back * up_proj * sigmoid * (1.0 + gate * (1.0 - sigmoid))
            hidden_t[0:FQ, to] = gate_rows.T.astype(BF16)
            hidden_t[FQ : 2 * FQ, to] = up_rows.T.astype(BF16)
            hidden_t[2 * FQ : 3 * FQ, to] = active.T.astype(BF16)

    def hidden_units(start, tall, chunks):
        for piece in range(PIECES):
            hidden_piece(start, tall, chunks, piece)
        hidden_end(start, tall)

    for copy in load_later:
        copy.wait()
    hidden_units(0, 2 * CHUNK, (0, 1))

    pass_rows(2, PIECES - 1)
    for piece in range(PIECES):
        share_rows(2, piece)

    for copy in kv_to_z:
        copy.wait()
    total = kv_y_sum[pl.ds(pl.multiple_of(z * 64, 64), 64), :].astype(F32)
    for step in range(7):
        total = total + kv_z[step].astype(F32)
    for lane in range(4):
        kv_out[:, lane * 128 : lane * 128 + 128] = total[lane * 16 : lane * 16 + 16, :]
    kv_to_core.wait_send()

    z_next[0].wait_recv()
    last = (2 * CHUNK + 256, 2 * CHUNK - 256)
    for piece in range(PIECES):
        z_next[1 + piece].wait_recv()
        send_rows(3, piece)
        if piece >= 1:
            hidden_piece(*last, (3,), piece - 1)
        pass_rows(3, piece)
        if piece == 0:
            hidden_units(2 * CHUNK, 256, (2,))
        share_rows(3, piece)
    hidden_piece(*last, (3,), PIECES - 1)
    hidden_end(*last)

    across, far_half = lax.rem(x + 2, 4), 1 - zl
    side = x // 2
    turns = [lax.rem(x + 1, 4), lax.rem(x + 3, 4)]

    def early(which):
        return pl.ds(pl.multiple_of(which * SLICE, 128), EARLY)

    def late(which, turn=None):
        at = which * SLICE + EARLY
        if turn is None:
            return pl.ds(pl.multiple_of(at, 128), LATE)
        return pl.ds(pl.multiple_of(at + turn * TURN, 64), TURN)

    low = lax.broadcasted_iota(jnp.int32, (384, 128), 1) < 64

    def gradients(pair):
        at = pl.ds(pl.multiple_of(pair * PAIR, 128), PAIR)
        work[0 : 2 * FQ, :] = jnp.dot(
            hidden_t[0 : 2 * FQ, :], rows[0, :, at], preferred_element_type=F32
        )
        work[2 * FQ : 3 * FQ, :] = jnp.dot(
            hidden_t[2 * FQ : 3 * FQ, :], rows[1, :, at], preferred_element_type=F32
        )
        start = pair * 2 * SLICE

        def put(which, block, value):
            to = pl.multiple_of(start + which * SLICE + block * 384, 128)
            parts[pl.ds(to, 384), :] = value.astype(BF16)

        for lane in range(3):
            for tall in range(2):
                high = slice(tall * 384, tall * 384 + 384)
                put(0, tall * 3 + lane, work[high, lane * 128 : lane * 128 + 128])
                put(1, tall * 3 + lane, work[high, 512 + lane * 128 : 640 + lane * 128])
        top, bottom = work[0:384, 384:512], pltpu.roll(work[384:768, 384:512], 64, 1)
        put(0, 6, jnp.where(low, top, bottom))
        put(1, 6, jnp.where(low, bottom, top))

    def onward_x(half):
        return lax.rem(x + 1 + 2 * half, 4)

    def back_x(half):
        return lax.rem(x + 3 + 2 * half, 4)

    def add_rows(start, count, tile_rows, *added):
        @pl.loop(0, count // tile_rows)
        def _(tile):
            at = pl.multiple_of(tile * tile_rows, 64)
            here = pl.ds(pl.multiple_of(start + at, 64), tile_rows)
            total = parts[here, :].astype(F32)
            for one in added:
                total = total + one[pl.ds(at, tile_rows), :].astype(F32)
            parts[here, :] = total.astype(BF16)

    sums_sent = []

    def send(src, dst, device):
        copy = remote(src, dst, device)
        copy.start()
        sums_sent.append(copy)
        return copy

    def send_zl(target):
        return send(parts.at[late(far_half * 4 + target)], late_zl.at[target], other_zl)

    def send_across(half):
        return send(
            parts.at[early(half * 4 + across)], early_first.at[half], at_x(onward_x(half))
        )

    zl_sent = {}
    gradients(far_half * 2 + 1 - side)
    for place in range(2):
        zl_sent[place] = send_zl((1 - side) * 2 + place)
    far_across = send_across(far_half)
    gradients(zl * 2 + 1 - side)
    near_across = send_across(zl)
    gradients(far_half * 2 + side)
    for place in range(2):
        zl_sent[2 + place] = send_zl(side * 2 + place)
    gradients(zl * 2 + side)
    plain = [
        send(
            parts.at[early(half * 4 + back_x(half))],
            early_sums.at[half, 1],
            at_x(back_x(half)),
        )
        for half in (far_half, zl)
    ]
    merged = []
    for half, copy in ((far_half, far_across), (zl, near_across)):
        copy.wait_recv()
        ahead = half * 4 + onward_x(half)
        add_rows(ahead * SLICE, EARLY, 384, early_first.at[half])
        merged.append(
            send(parts.at[early(ahead)], early_sums.at[half, 0], at_x(onward_x(half)))
        )

    for copy in zl_sent.values():
        copy.wait_recv()

    def take_zl(target):
        add_rows((zl * 4 + target) * SLICE + EARLY, LATE, 384, late_zl.at[target])

    def turn_rows(turn):
        return pl.ds(turn * TURN, TURN)

    take_zl(across)
    late_across = [
        send(
            parts.at[late(zl * 4 + across, turn)], late_first.at[turn_rows(turn)], at_x(turns[turn])
        )
        for turn in range(2)
    ]
    for target in turns:
        take_zl(target)
    late_plain = [
        send(
            parts.at[late(zl * 4 + turns[1 - turn], turn)],
            late_sums.at[1, turn_rows(turn)],
            at_x(turns[1 - turn]),
        )
        for turn in range(2)
    ]
    take_zl(x)

    for copy in (plain[0], merged[0]):
        copy.wait_recv()
    here = far_half * 4 + x
    add_rows(
        here * SLICE, EARLY, 384, early_sums.at[far_half, 0], early_sums.at[far_half, 1]
    )
    early_last = send(parts.at[early(here)], early_zl, other_zl)

    late_merged = []
    for turn in range(2):
        late_across[turn].wait_recv()
        ahead = zl * 4 + turns[turn]
        add_rows(
            ahead * SLICE + EARLY + turn * TURN, TURN, 192, late_first.at[turn_rows(turn)]
        )
        late_merged.append(
            send(
                parts.at[late(ahead, turn)], late_sums.at[0, turn_rows(turn)], at_x(turns[turn])
            )
        )

    mine_at = (zl * 4 + x) * SLICE

    def put_sum(block, added):
        total = parts[pl.ds(pl.multiple_of(mine_at + block * 384, 128), 384), :].astype(F32)
        for one in added:
            total = total + one.astype(F32)
        work[0:384, block * 128 : block * 128 + 128] = total

    for copy in (plain[1], merged[1], early_last):
        copy.wait_recv()
    for block in range(4):
        at = pl.ds(block * 384, 384)
        put_sum(block, (early_sums[zl, 0, at, :], early_sums[zl, 1, at, :], early_zl[at, :]))
    for copy in late_plain + late_merged:
        copy.wait_recv()
    for block in range(3):
        at = pl.ds(block * 384, 384)
        put_sum(4 + block, (late_sums[0, at, :], late_sums[1, at, :]))

    odd = lax.rem(x, 2)
    main = pl.ds(pl.multiple_of(384 + odd * 64, 64), 384)
    edge = pl.ds(pl.multiple_of(768 - odd * 384, 64), 64)
    edges = work[0:384, 768:896].T
    swapped = lax.broadcasted_iota(jnp.int32, (64, 384), 0) * 0 + odd == 1
    work[edge, 0:384] = jnp.where(swapped, edges[64:128, :], edges[0:64, :])
    work[edge, 384:768] = jnp.where(swapped, edges[0:64, :], edges[64:128, :])
    for tall in range(2):
        high = slice(tall * 384, tall * 384 + 384)
        work[main, high] = work[0:384, high].T
    store = local(work.at[pl.ds(384, 448), pl.ds(0, 768)], sums_out)
    store.start()

    for copy in [swap_meta] + sums_sent:
        copy.wait_send()
    for copy in z_near + z_far + z_next:
        copy.wait_send()
    for chunk in range(4):
        for piece in range(PIECES):
            if chunk >= 2:
                for copy in y_sent[chunk, piece]:
                    copy.wait_send()
            y_passed[chunk, piece].wait_send()
            core_sent[chunk, piece].wait_send()
    store.wait()


def run_kernel(ids, probs, gain, *arrays):
    vmem, any_space = pl.BlockSpec(memory_space=pltpu.VMEM), pl.BlockSpec(memory_space=pl.ANY)
    return pl.pallas_call(
        kernel,
        out_shape=(
            jax.ShapeDtypeStruct((16, KVL), F32),
            jax.ShapeDtypeStruct((448, 3 * FQ), F32),
        ),
        in_specs=[vmem] * 2 + [any_space] * (1 + len(arrays)),
        out_specs=(vmem, any_space),
        scratch_shapes=[
            pltpu.VMEM((2, TOK, D), BF16),
            pltpu.VMEM((4, 2 * TOK, D), BF16),
            pltpu.VMEM((4, 2, 16, TOK), F32),
            pltpu.VMEM((2, 3, BLOCK, D), BF16),
            pltpu.VMEM((4, BLOCK, D), BF16),
            pltpu.VMEM((2, ROWS, D), BF16),
            pltpu.VMEM((D, 2 * FQ), BF16),
            pltpu.VMEM((FQ, D), BF16),
            pltpu.VMEM((TOK, KVL), BF16),
            pltpu.VMEM((1, D), F32),
            pltpu.VMEM((3 * FQ, ROWS), BF16),
            pltpu.VMEM((904, PAIR), F32),
            pltpu.VMEM((8 * SLICE, 128), BF16),
            pltpu.VMEM((2, EARLY, 128), BF16),
            pltpu.VMEM((2, 2, EARLY, 128), BF16),
            pltpu.VMEM((EARLY, 128), BF16),
            pltpu.VMEM((4, LATE, 128), BF16),
            pltpu.VMEM((LATE, 128), BF16),
            pltpu.VMEM((2, LATE, 128), BF16),
            pltpu.VMEM((8192, 128), BF16),
            pltpu.VMEM((3, 2048, 128), BF16),
            pltpu.VMEM((2048, 128), BF16),
            pltpu.VMEM((3, 512, 128), BF16),
            pltpu.VMEM((512, 128), BF16),
            pltpu.VMEM((7, 64, 128), BF16),
            pltpu.SemaphoreType.DMA((COPIES,)),
            pltpu.SemaphoreType.DMA((COPIES,)),
            pltpu.SemaphoreType.DMA((16,)),
        ],
        compiler_params=pltpu.CompilerParams(
            collective_id=0, has_side_effects=True, vmem_limit_bytes=63 << 20
        ),
        cost_estimate=pl.CostEstimate(
            flops=2 * ROWS * D * FQ * 6, bytes_accessed=12 << 20, transcendentals=ROWS * FQ
        ),
        name="expert_gradients",
    )(ids, probs, gain, *arrays)


def body(
    attn_input,
    kv_gain,
    latent_cot,
    attn_resid,
    moe_input,
    moe_cot,
    expert_ids,
    gate_probs,
    w_gate,
    w_up,
    w_down,
    gate_resid,
    up_resid,
    down_resid,
):
    latent_sum, sums = run_kernel(
        expert_ids.T,
        gate_probs.T,
        kv_gain,
        moe_input,
        moe_cot,
        attn_input,
        latent_cot,
        w_gate,
        w_up,
        w_down,
    )
    kv_grad = (latent_sum[:14] + attn_resid).astype(BF16)
    gate_grad = (sums[:, :FQ] + gate_resid).astype(BF16)
    up_grad = (sums[:, FQ : 2 * FQ] + up_resid).astype(BF16)
    down_grad = (sums[:, 2 * FQ :] + down_resid.T).astype(BF16).T
    return (kv_grad, gate_grad, up_grad, down_grad)


def solution(mesh):
    torus = Mesh(mesh.devices.reshape(2, 4, 4, 4, 2), ("edp_0", "edp_1", "ep_0", "ep_1", "ep_2"))
    return jax.shard_map(
        body,
        mesh=torus,
        in_specs=(
            P(EDP_EP, None),
            P(),
            P(EDP_EP, None),
            P(EDP_EP, None),
            P(EDP_EP, None),
            P(EDP_EP, None),
            P(EDP_EP, None),
            P(EDP_EP, None),
            P(None, EP),
            P(None, EP),
            P(EP, None),
            P(EDP, EP),
            P(EDP, EP),
            P(EP, EDP),
        ),
        out_specs=(P(EDP_EP, None), P(EDP, EP), P(EDP, EP), P(EP, EDP)),
        check_vma=False,
    )
```
